256 devices in a mesh: dp: 32 (over z, x_hi, core), fsdp: 8 (over x_lo, y).
Axes of the slice: x: 4 (x_hi: 2, x_lo: 2; x = x_hi * 2 + x_lo), y: 4, z: 8, core: 2. Of those that a mesh axis runs over, the one named last changes fastest.
Arguments:
- query_rows: bfloat16 [32768, 2048], P(('dp', 'fsdp')), may hold values from -12 to 12
- key_rows: bfloat16 [32768, 2048], P(('dp', 'fsdp')), may hold values from -12 to 12
- value_rows: bfloat16 [32768, 2048], P(('dp', 'fsdp')), may hold values from -6 to 6
- out_grad: bfloat16 [32768, 2048], P(('dp', 'fsdp')), may hold values from -6 to 6
- params: float32 [65536, 2048], P(('dp', 'fsdp')), may hold values from -6 to 6
- momentum: float32 [65536, 2048], P(('dp', 'fsdp')), may hold values from -3 to 3
- token_ids: int32 [32768], P(('dp', 'fsdp')), may hold values from 0 to 8191
- block_mask: int32 [8, 8], replicated, may hold values from 0 to 1, as said below
- step_index: int32 [1], replicated, may hold values from 0 to 7
Outputs:
- grad_query: bfloat16 [32768, 2048], P(('dp', 'fsdp'))
- grad_key: bfloat16 [32768, 2048], P(('dp', 'fsdp'))
- grad_value: bfloat16 [32768, 2048], P(('dp', 'fsdp'))
- new_params: float32 [65536, 2048], P(('dp', 'fsdp'))
- new_momentum: float32 [65536, 2048], P(('dp', 'fsdp'))
The draws below stay inside these ranges and needn't reach their ends.
Inputs may be any that keep to these rules, and one draw needn't show every extreme that they name: block_mask[i, i] is 1 and block_mask[i, j] is 0 for j > i.
All inputs are finite; a program needn't handle non-finite values.
Results may differ from the reference program's by a relative error of at most 0.0095.
Values may be sent and summed in bfloat16 or wider, within the bound.
A program may use at most 128 MiB of HBM per device.

```python
import math
import jax
import jax.numpy as jnp
from jax import lax

D = 2048
HEADS = 16
HD = 128
STEMS = 4
CODES = 2048
BLOCK = 128
INNER = 2048
TOKENS = 1024
NB = 8
ALL_TOKENS = 32768
ALL_INNER = 65536
N_DP = 32


def paired_rows(key):
    base_key = jax.random.fold_in(key, 7301)
    query_part = jnp.clip(jax.random.normal(jax.random.fold_in(base_key, 1), (ALL_TOKENS, INNER), jnp.float32), -6.0, 6.0)
    key_part = jnp.clip(jax.random.normal(jax.random.fold_in(base_key, 2), (ALL_TOKENS, INNER), jnp.float32), -6.0, 6.0)
    return (query_part, key_part)


def draw_query_rows(key, part):
    return paired_rows(key)[0].astype(jnp.bfloat16)


def draw_key_rows(key, part):
    return paired_rows(key)[1].astype(jnp.bfloat16)


def draw_block_mask(key, part):
    coin_flips = jax.random.randint(jax.random.fold_in(key, 4409), (NB, NB), 0, 2, dtype=jnp.int32)
    row_index = jnp.arange(NB, dtype=jnp.int32)[:, None]
    col_index = jnp.arange(NB, dtype=jnp.int32)[None, :]
    return jnp.where(row_index == col_index, 1, jnp.where(col_index < row_index, coin_flips, 0)).astype(jnp.int32)


def place_ends(values, own_key, smallest, top_value):
    dims = values.shape
    spot = [jax.random.randint(jax.random.fold_in(own_key, axis), (), 0, dims[axis]) for axis in range(len(dims))]
    values = values.at[tuple(spot)].set(smallest)
    longest = dims.index(max(dims))
    spot[longest] = (spot[longest] + 1) % dims[longest]
    return values.at[tuple(spot)].set(top_value)


def levels(rng, dims, cuts, smallest, top_value):
    def one(dim, parts):
        draws = jax.random.uniform(jax.random.fold_in(jax.random.fold_in(rng, 6), dim), (parts,), jnp.float32, smallest / len(cuts), top_value / len(cuts))
        return jnp.repeat(jnp.exp(draws), dims[dim] // parts).reshape((-1,) + (1,) * (len(dims) - dim - 1))

    loudness = one(*cuts[0])
    for cut in cuts[1:]:
        loudness = loudness * one(*cut)
    return loudness


def centred(stream_key, extent, deviation, bound, cuts=(), kind=jnp.bfloat16):
    factor_of = levels(stream_key, extent, cuts, -0.22, 0.18) if cuts else 1.0
    drawn = jax.random.normal(stream_key, extent, jnp.float32) * deviation * factor_of
    return jnp.minimum(jnp.maximum(drawn, -bound), bound).astype(kind)


def setup_inputs(seed: int = 0) -> dict:
    streams_of = jax.random.split(jax.random.key(seed), 10)
    query_rows = draw_query_rows(jax.random.fold_in(streams_of[9], 71), 0)
    key_rows = draw_key_rows(jax.random.fold_in(streams_of[9], 71), 0)
    value_rows = centred(streams_of[2], (ALL_TOKENS, INNER), 1.0, 6.0, ((0, 256),))
    out_grad = centred(streams_of[3], (ALL_TOKENS, D), 1.0, 6.0, ((0, 256),))
    params = centred(streams_of[4], (ALL_INNER, D), 1.0, 6.0, ((0, 256),), jnp.float32)
    momentum = centred(streams_of[5], (ALL_INNER, D), 0.5, 3.0, ((0, 256),), jnp.float32)
    token_ids = place_ends(jax.random.randint(streams_of[6], (ALL_TOKENS,), 0, STEMS * CODES), jax.random.fold_in(streams_of[6], 1), 0, (STEMS * CODES) - 1).astype(jnp.int32)
    block_mask = draw_block_mask(jax.random.fold_in(streams_of[9], 71), 0)
    step_index = jax.random.randint(streams_of[8], (1,), 0, 8).astype(jnp.int32)
    return {"query_rows": query_rows, "key_rows": key_rows, "value_rows": value_rows, "out_grad": out_grad, "params": params, "momentum": momentum, "token_ids": token_ids, "block_mask": block_mask, "step_index": step_index}


MOMENTUM_RATE = 0.9
LEARN_RATE = 0.25

def rounded(values):
    return lax.optimization_barrier(values.astype(jnp.bfloat16)).astype(jnp.float32)

def replica_step(query_rows, key_rows, value_rows, out_grad, params, momentum, token_ids, block_mask, step_value):
    inv_width = 1.0 / math.sqrt(INNER)
    score_scale = 1.0 / math.sqrt(HD)
    weight16 = rounded(params)
    grad_out32 = out_grad.astype(jnp.float32)
    grad_attn = rounded(jnp.dot(grad_out32, weight16.T, preferred_element_type=jnp.float32) * inv_width)
    position = jnp.arange(TOKENS, dtype=jnp.int32)
    block_of = position // BLOCK
    spread = block_mask[block_of[:, None], block_of[None, :]]
    stem_ids = token_ids // CODES
    allowed = (spread == 1) & (position[None, :] <= position[:, None]) & ((stem_ids[:, None] == stem_ids[None, :]) | (block_of[:, None] == block_of[None, :]))
    query_h = query_rows.astype(jnp.float32).reshape(TOKENS, HEADS, HD)
    key_h = key_rows.astype(jnp.float32).reshape(TOKENS, HEADS, HD)
    value_h = value_rows.astype(jnp.float32).reshape(TOKENS, HEADS, HD)
    grad_h = grad_attn.reshape(TOKENS, HEADS, HD)
    scores = jnp.einsum('qhd,khd->hqk', query_h, key_h) * score_scale
    scores = jnp.where(allowed[None], scores, -1e+30)
    top_score = lax.optimization_barrier(jnp.max(scores, axis=-1, keepdims=True))
    exp_terms = jnp.where(allowed[None], jnp.exp(scores - top_score), 0.0)
    prob_f32 = exp_terms / lax.optimization_barrier(jnp.sum(exp_terms, axis=-1, keepdims=True))
    prob_b16 = rounded(prob_f32)
    attended = rounded(jnp.einsum('hqk,khd->qhd', prob_b16, value_h)).reshape(TOKENS, INNER)
    grad_value = jnp.einsum('hqk,qhd->khd', prob_b16, grad_h).reshape(TOKENS, INNER)
    grad_prob = jnp.einsum('qhd,khd->hqk', grad_h, value_h)
    row_dot = lax.optimization_barrier(jnp.sum(prob_f32 * grad_prob, axis=-1, keepdims=True))
    grad_score = rounded(prob_f32 * (grad_prob - row_dot) * score_scale)
    grad_query = jnp.einsum('hqk,khd->qhd', grad_score, key_h).reshape(TOKENS, INNER)
    grad_key = jnp.einsum('hqk,qhd->khd', grad_score, query_h).reshape(TOKENS, INNER)
    grad_weight = jnp.dot(attended.T, grad_out32, preferred_element_type=jnp.float32) * inv_width
    moment = MOMENTUM_RATE * momentum + grad_weight
    correction = 1.0 / (1.0 - jnp.exp((step_value + 1).astype(jnp.float32) * math.log(MOMENTUM_RATE)))
    stepped = params - LEARN_RATE * correction * moment
    return (grad_query.astype(jnp.bfloat16), grad_key.astype(jnp.bfloat16), grad_value.astype(jnp.bfloat16), stepped, moment)

def reference(query_rows, key_rows, value_rows, out_grad, params, momentum, token_ids, block_mask, step_index):
    step_value = step_index[0]

    def per_replica(pieces):
        return replica_step(pieces[0], pieces[1], pieces[2], pieces[3], pieces[4], pieces[5], pieces[6], block_mask, step_value)
    stacked = (query_rows.reshape(N_DP, TOKENS, INNER), key_rows.reshape(N_DP, TOKENS, INNER), value_rows.reshape(N_DP, TOKENS, INNER), out_grad.reshape(N_DP, TOKENS, D), params.reshape(N_DP, INNER, D), momentum.reshape(N_DP, INNER, D), token_ids.reshape(N_DP, TOKENS))
    grad_query, grad_key, grad_value, stepped, moment = lax.map(per_replica, stacked)
    replica_ids = jnp.arange(N_DP, dtype=jnp.int32)
    partner = jnp.bitwise_xor(replica_ids, jnp.left_shift(jnp.int32(1), step_value % 4)).astype(jnp.int32)
    new_params = 0.5 * (stepped + stepped[partner])
    new_momentum = 0.5 * (moment + moment[partner])
    return (grad_query.reshape(ALL_TOKENS, INNER), grad_key.reshape(ALL_TOKENS, INNER), grad_value.reshape(ALL_TOKENS, INNER), new_params.reshape(ALL_INNER, D), new_momentum.reshape(ALL_INNER, D))
```

```python
import functools
import math

import jax
import jax.numpy as jnp
from jax import lax
from jax.experimental import pallas as pl
from jax.experimental.pallas import tpu as pltpu
from jax.sharding import PartitionSpec as P

HD = 128
INNER = 2048
MOMENTUM_RATE = 0.9
LEARN_RATE = 0.25
MESH = pl.DeviceIdType.MESH
NEG = -1e30
BF = jnp.bfloat16
F32 = jnp.float32
CT_MINOR = (((1,), (1,)), ((), ()))
CT_MAJOR = (((0,), (0,)), ((), ()))
CT_PLAIN = (((1,), (0,)), ((), ()))


def dot(a, b, dims):
    return lax.dot_general(a, b, dims, preferred_element_type=F32)


def kernel(
    bit, top,
    bm, q, k, v, og, params, mom, ids,
    dq, dk, dv, mo, pr, mr,
    qb, kb, vb, ogb, pf, mf, w16, m16, idb, skc, bias, pt, att, gr, dqb, dkb, dvb, dka, dva,
    ag_s, ag_r, a2a_s, a2a_r, id_s, id_r, bk_s, bk_r, px_s, px_r, loc,
):
    f = lax.axis_index("fsdp")
    d = lax.axis_index("dp")
    x = f // 4
    y = lax.rem(f, 4)

    def member(r):
        return lax.rem(x + r // 4, 2) * 4 + lax.rem(y + r % 4, 4)

    def back(r):
        return lax.rem(x + r // 4, 2) * 4 + lax.rem(y + 4 - r % 4, 4)

    width = 1 << bit
    partner = d + width - 2 * width * lax.rem(d // width, 2)
    to_partner = {"dp": partner}

    def rows(block, start=0, size=128):
        return pl.ds(pl.multiple_of(block * 128 + start, 16), size)

    def remote(src, dst, s_sem, r_sem, device):
        return pltpu.make_async_remote_copy(
            src_ref=src, dst_ref=dst, send_sem=s_sem, recv_sem=r_sem, device_id=device, device_id_type=MESH
        )

    own_rows = rows(f)
    locals_in = [
        pltpu.make_async_copy(params, pf, loc.at[0]),
        pltpu.make_async_copy(mom, mf, loc.at[1]),
        pltpu.make_async_copy(ids, idb.at[f], loc.at[2]),
    ]
    own_cols = pl.ds(pl.multiple_of(f * 256, 256), 256)
    for n, (src, dst) in enumerate(((q, qb), (k, kb), (v, vb))):
        locals_in.append(pltpu.make_async_copy(src.at[:, own_cols], dst.at[own_rows, :], loc.at[3 + n]))
    locals_in.append(pltpu.make_async_copy(og, ogb.at[own_rows, :], loc.at[6]))
    for copy in locals_in:
        copy.start()

    barrier = pltpu.get_barrier_semaphore()
    for r in range(1, 8):
        pl.semaphore_signal(barrier, inc=1, device_id={"fsdp": member(r)}, device_id_type=MESH)
    pl.semaphore_signal(barrier, inc=1, device_id=to_partner, device_id_type=MESH)
    pl.semaphore_wait(barrier, 8)

    n_x = {"fsdp": member(4)}
    y_p = {"fsdp": member(1)}
    y_m = {"fsdp": member(3)}
    sent = []

    def gather_send(n, block, start, size, device):
        part = ogb.at[rows(block, start, size), :]
        src = og if n < 3 else part
        copy = remote(src, part, ag_s.at[n], ag_r.at[n], device)
        copy.start()
        sent.append(copy)

    def gather_wait(n, block, start, size):
        part = ogb.at[rows(block, start, size), :]
        remote(part, part, ag_s.at[n], ag_r.at[n], n_x).wait_recv()

    for r in range(1, 8):
        copy = remote(ids, idb.at[f], id_s.at[r], id_r.at[r], {"fsdp": member(r)})
        copy.start()
        sent.append(copy)
    gather_send(0, f, 0, 128, n_x)
    gather_send(1, f, 0, 128, y_p)
    gather_send(2, f, 0, 128, y_m)

    for n, (src, dst) in enumerate(((q, qb), (k, kb), (v, vb))):
        for r in range(1, 8):
            g = member(r)
            cols = pl.ds(pl.multiple_of(g * 256, 256), 256)
            copy = remote(src.at[:, cols], dst.at[own_rows, :], a2a_s.at[n, r], a2a_r.at[n, r], {"fsdp": g})
            copy.start()
            sent.append(copy)

    locals_in[0].wait()

    def to_w16(n, _):
        part = pl.ds(pl.multiple_of(n * 32, 32), 32)
        w16[part, :] = pf[part, :].astype(BF)
        return 0

    lax.fori_loop(0, 8, to_w16, 0)
    locals_in[1].wait()
    locals_in[2].wait()
    for r in range(1, 8):
        remote(ids, idb.at[back(r)], id_s.at[r], id_r.at[r], n_x).wait_recv()

    def stem_col(g, _):
        stem = lax.shift_right_logical(idb[g], 11).astype(F32)
        spread = jnp.broadcast_to(stem, (128, 128))
        skc[pl.ds(pl.multiple_of(g * 128, 128), 128), :] = spread.T
        return 0

    lax.fori_loop(0, 8, stem_col, 0)
    swap_p = remote(w16, pr, px_s.at[0], px_r.at[0], to_partner)
    swap_p.start()

    iota_k = lax.broadcasted_iota(jnp.int32, (128, 128), 0)
    iota_q = lax.broadcasted_iota(jnp.int32, (128, 128), 1)
    tri = jnp.where(iota_k <= iota_q, 0.0, NEG).astype(F32)

    def bias_row(kg, _):
        k_rows = pl.ds(pl.multiple_of(kg * 128, 128), 128)
        sk = skc[k_rows, :]
        bias[k_rows, k_rows] = tri

        def bias_tile(qg, _):
            sq = lax.shift_right_logical(idb[qg], 11).astype(F32)
            sq = sq + (1 - bm[qg, kg]).astype(F32) * 16.0
            bias[k_rows, pl.ds(pl.multiple_of(qg * 128, 128), 128)] = jnp.where(sk == sq, 0.0, NEG)
            return 0

        lax.fori_loop(kg + 1, 8, bias_tile, 0)
        return 0

    lax.fori_loop(0, 8, bias_row, 0)
    for ip in range(4):
        bias[256 * ip + 128 : 256 * ip + 256, 256 * ip : 256 * ip + 128] = jnp.full((128, 128), NEG, F32)

    inv_width = 1.0 / math.sqrt(INNER)
    scale = 1.0 / math.sqrt(HD)
    scale2 = scale * math.log2(math.e)

    def grad_block(block):
        at = rows(block)
        gr[at, :] = (dot(ogb[at, :], w16[...], CT_MINOR) * inv_width).astype(BF)

    locals_in[6].wait()
    grad_block(f)

    gather_wait(0, member(4), 0, 128)
    gather_wait(1, member(3), 0, 128)
    gather_wait(2, member(1), 0, 128)
    gather_send(3, member(1), 0, 64, y_m)
    gather_send(4, member(3), 64, 64, y_p)
    gather_send(5, member(4), 0, top, y_p)
    gather_send(6, member(4), 0, top, y_m)
    if top < 128:
        gather_send(7, member(1), top, 128 - top, n_x)
        gather_send(8, member(3), top, 128 - top, n_x)
    grad_block(member(4))
    grad_block(member(1))
    grad_block(member(3))

    for n, (src, dst) in enumerate(((q, qb), (k, kb), (v, vb))):
        locals_in[3 + n].wait()
        for r in range(1, 8):
            land = dst.at[rows(back(r)), :]
            remote(land, land, a2a_s.at[n, r], a2a_r.at[n, r], n_x).wait_recv()

    def forward(ip):
        size = 256 * (ip + 1)
        here = slice(256 * ip, 256 * ip + 256)

        def head(h, _):
            hs = pl.ds(pl.multiple_of(h * 128, 128), 128)
            s = dot(kb[0:size, hs], qb[here, hs], CT_MINOR) * scale2 + bias[0:size, here]
            e = jnp.exp2(s - jnp.max(s, axis=0, keepdims=True))
            p = (e * (1.0 / jnp.sum(e, axis=0, keepdims=True))).astype(BF)
            pt[h, 0:size, here] = p
            att[hs, here] = dot(vb[0:size, hs], p, CT_MAJOR).astype(BF)
            return 0

        lax.fori_loop(0, 2, head, 0)

    half = top // 2
    forward(0)
    forward(1)
    gather_wait(3, member(2), 0, 64)
    gather_wait(4, member(2), 64, 64)
    if top < 128:
        gather_send(9, member(2), top, 128 - top, n_x)
    gather_wait(5, member(7), 0, top)
    gather_send(10, member(7), half, top - half, y_p)
    gather_wait(6, member(5), 0, top)
    gather_send(11, member(5), 0, half, y_m)
    forward(2)
    forward(3)
    grad_block(member(2))
    if top < 128:
        gather_wait(7, member(5), top, 128 - top)
        gather_wait(8, member(7), top, 128 - top)
    grad_block(member(5))
    grad_block(member(7))
    gather_wait(10, member(6), half, top - half)
    gather_wait(11, member(6), 0, half)
    if top < 128:
        gather_wait(9, member(6), top, 128 - top)

    def weight_cols(n, _):
        cols = pl.ds(pl.multiple_of(n * 256, 256), 256)
        moment = MOMENTUM_RATE * mf[:, cols] + dot(att[...], ogb[:, cols], CT_PLAIN) * inv_width
        mf[:, cols] = moment
        m16[:, cols] = moment.astype(BF)
        return 0

    lax.fori_loop(0, 8, weight_cols, 0)
    grad_block(member(6))
    swap_m = remote(m16, mr, px_s.at[1], px_r.at[1], to_partner)
    swap_m.start()
    out_m = pltpu.make_async_copy(mf, mo, loc.at[7])
    out_m.start()

    def backward(ip):
        size = 256 * (ip + 1)
        here = slice(256 * ip, 256 * ip + 256)

        def head(h, _):
            hs = pl.ds(pl.multiple_of(h * 128, 128), 128)
            g = gr[here, hs]
            p16 = pt[h, 0:size, here]
            p = p16.astype(F32)
            dp = dot(vb[0:size, hs], g, CT_MINOR)
            row_dot = jnp.sum(p * dp, axis=0, keepdims=True)
            ds = (p * (dp - row_dot) * scale).astype(BF)
            dv_part = dot(p16, g, CT_PLAIN)
            dk_part = dot(ds, qb[here, hs], CT_PLAIN)
            if ip == 3:
                dva[0:size, hs] = dv_part
                dka[0:size, hs] = dk_part
            else:
                dva[0:size, hs] += dv_part
                dka[0:size, hs] += dk_part
            dqb[here, hs] = dot(ds, kb[0:size, hs], CT_MAJOR).astype(BF)
            return 0

        lax.fori_loop(0, 2, head, 0)

    for ip in (3, 2, 1, 0):
        backward(ip)

    def finish(n, _):
        part = pl.ds(pl.multiple_of(n * 128, 128), 128)
        dkb[part, :] = dka[part, :].astype(BF)
        dvb[part, :] = dva[part, :].astype(BF)
        return 0

    lax.fori_loop(0, 8, finish, 0)
    outs = []
    for n, (src, dst) in enumerate(((dqb, dq), (dkb, dk), (dvb, dv))):
        for r in range(1, 8):
            g = member(r)
            copy = remote(src.at[rows(g), :], dst.at[:, own_cols], bk_s.at[n, r], bk_r.at[n, r], {"fsdp": g})
            copy.start()
            sent.append(copy)
        copy = pltpu.make_async_copy(src.at[own_rows, :], dst.at[:, own_cols], loc.at[8 + n])
        copy.start()
        outs.append(copy)
    for copy in sent:
        copy.wait_send()
    for n, (src, dst) in enumerate(((dqb, dq), (dkb, dk), (dvb, dv))):
        for r in range(1, 8):
            cols = pl.ds(pl.multiple_of(back(r) * 256, 256), 256)
            remote(src.at[own_rows, :], dst.at[:, cols], bk_s.at[n, r], bk_r.at[n, r], n_x).wait_recv()
    for copy in outs:
        copy.wait()
    out_m.wait()
    swap_p.wait()
    swap_m.wait()


def fused(bit, bm, q, k, v, og, params, mom, ids):
    anyspace = pl.BlockSpec(memory_space=pl.ANY)
    tok = jax.ShapeDtypeStruct((128, INNER), BF)
    dma = pltpu.SemaphoreType.DMA
    heads = pltpu.VMEM((1024, 256), BF)
    return pl.pallas_call(
        functools.partial(kernel, bit, 128 if bit == 1 else 64),
        name=f"step_{bit}",
        out_shape=(
            tok, tok, tok,
            jax.ShapeDtypeStruct((256, INNER), F32),
            jax.ShapeDtypeStruct((256, INNER), BF),
            jax.ShapeDtypeStruct((256, INNER), BF),
        ),
        in_specs=[pl.BlockSpec(memory_space=pltpu.SMEM)] + [anyspace] * 7,
        out_specs=(anyspace,) * 6,
        scratch_shapes=[
            heads, heads, heads,
            pltpu.VMEM((1024, INNER), BF),
            pltpu.VMEM((256, INNER), F32),
            pltpu.VMEM((256, INNER), F32),
            pltpu.VMEM((256, INNER), BF),
            pltpu.VMEM((256, INNER), BF),
            pltpu.VMEM((8, 1, 128), jnp.int32),
            pltpu.VMEM((1024, 128), F32),
            pltpu.VMEM((1024, 1024), F32),
            pltpu.VMEM((2, 1024, 1024), BF),
            pltpu.VMEM((256, 1024), BF),
            heads, heads, heads, heads,
            pltpu.VMEM((1024, 256), F32),
            pltpu.VMEM((1024, 256), F32),
            dma((12,)), dma((12,)), dma((3, 8)), dma((3, 8)), dma((8,)), dma((8,)),
            dma((3, 8)), dma((3, 8)), dma((2,)), dma((2,)), dma((11,)),
        ],
        compiler_params=pltpu.CompilerParams(
            collective_id=bit, has_side_effects=True, vmem_limit_bytes=60 * 1024 * 1024
        ),
    )(bm, q, k, v, og, params, mom, ids)


def shards(q, k, v, og, params, mom, token_ids, block_mask, step_index):
    step_value = step_index[0]
    correction = 1.0 / (1.0 - jnp.exp((step_value + 1).astype(F32) * math.log(MOMENTUM_RATE)))
    rate = LEARN_RATE * correction
    ids = token_ids.reshape(1, 128)
    dq, dk, dv, moment, other_p, other_m = lax.switch(
        step_value % 4,
        [functools.partial(fused, bit) for bit in range(4)],
        block_mask, q, k, v, og, params, mom, ids,
    )
    other_m = other_m.astype(F32)
    new_params = 0.5 * ((params - rate * moment) + (other_p.astype(F32) - rate * other_m))
    new_momentum = 0.5 * (moment + other_m)
    return dq, dk, dv, new_params, new_momentum


def solution(mesh):
    split = P(("dp", "fsdp"), None)
    return jax.shard_map(
        shards,
        mesh=mesh,
        in_specs=(split,) * 6 + (P(("dp", "fsdp")), P(), P()),
        out_specs=(split,) * 5,
        check_vma=False,
    )
```

```python
import functools
import math

import jax
import jax.numpy as jnp
from jax import lax
from jax.experimental import pallas as pl
from jax.experimental.pallas import tpu as pltpu
from jax.sharding import PartitionSpec as P

HD = 128
INNER = 2048
MOMENTUM_RATE = 0.9
LEARN_RATE = 0.25
MESH = pl.DeviceIdType.MESH
NEG = -1e30
BF = jnp.bfloat16
F32 = jnp.float32
CT_MINOR = (((1,), (1,)), ((), ()))
CT_MAJOR = (((0,), (0,)), ((), ()))
CT_PLAIN = (((1,), (0,)), ((), ()))


def dot(a, b, dims):
    return lax.dot_general(a, b, dims, preferred_element_type=F32)


def kernel(
    bit, top,
    bm, q, k, v, og, params, mom, ids,
    dq, dk, dv, pf, mf, pr, mr,
    qb, kb, vb, ogb, w16, m16, idb, skc, bias, pt, att, gr, dqb, dkb, dvb, dka, dva,
    ag_s, ag_r, a2a_s, a2a_r, id_s, id_r, bk_s, bk_r, px_s, px_r, loc,
):
    f = lax.axis_index("fsdp")
    d = lax.axis_index("dp")
    x = f // 4
    y = lax.rem(f, 4)

    def member(r):
        return lax.rem(x + r // 4, 2) * 4 + lax.rem(y + r % 4, 4)

    def back(r):
        return lax.rem(x + r // 4, 2) * 4 + lax.rem(y + 4 - r % 4, 4)

    width = 1 << bit
    partner = d + width - 2 * width * lax.rem(d // width, 2)
    to_partner = {"dp": partner}

    def rows(block, start=0, size=128):
        return pl.ds(pl.multiple_of(block * 128 + start, 16), size)

    def head_cols(block, h):
        return pl.ds(pl.multiple_of(block * 256 + h * 128, 128), 128)

    def remote(src, dst, s_sem, r_sem, device):
        return pltpu.make_async_remote_copy(
            src_ref=src, dst_ref=dst, send_sem=s_sem, recv_sem=r_sem, device_id=device, device_id_type=MESH
        )

    own_rows = rows(f)
    arrays = ((q, qb), (k, kb), (v, vb))
    results = ((dqb, dq), (dkb, dk), (dvb, dv))
    in_p = pltpu.make_async_copy(params, pf, loc.at[0])
    in_m = pltpu.make_async_copy(mom, mf, loc.at[1])
    in_id = pltpu.make_async_copy(ids, idb.at[f], loc.at[2])
    in_og = pltpu.make_async_copy(og, ogb.at[own_rows, :], loc.at[3])

    def in_head(n, h):
        src, dst = arrays[n]
        return pltpu.make_async_copy(src.at[:, head_cols(f, h)], dst.at[h, own_rows, :], loc.at[4 + 2 * n + h])

    for copy in (in_p, in_m, in_id, in_og):
        copy.start()
    for n in range(3):
        for h in range(2):
            in_head(n, h).start()

    barrier = pltpu.get_barrier_semaphore()
    for r in range(1, 8):
        pl.semaphore_signal(barrier, inc=1, device_id={"fsdp": member(r)}, device_id_type=MESH)
    pl.semaphore_signal(barrier, inc=1, device_id=to_partner, device_id_type=MESH)
    in_p.wait()

    def to_w16(n, _):
        part = pl.ds(pl.multiple_of(n * 32, 32), 32)
        w16[part, :] = pf[part, :].astype(BF)
        return 0

    lax.fori_loop(0, 8, to_w16, 0)
    pl.semaphore_wait(barrier, 8)

    n_x = {"fsdp": member(4)}
    y_p = {"fsdp": member(1)}
    y_m = {"fsdp": member(3)}
    all_rows = (0, 128)
    all_cols = (0, INNER)

    def gather(n, block, span, cols, device):
        part = ogb.at[rows(block, *span), pl.ds(cols[0], cols[1])]
        return remote(og if n < 3 else part, part, ag_s.at[n], ag_r.at[n], device)

    gathers = [
        (0, 0, all_rows, all_cols, n_x), (1, 0, all_rows, all_cols, y_p), (2, 0, all_rows, all_cols, y_m),
        (3, 1, (0, 64), all_cols, y_m), (4, 3, (64, 64), all_cols, y_p),
        (5, 4, all_rows, (0, top), y_p), (6, 4, all_rows, (0, top), y_m),
        (7, 1, all_rows, (top, INNER - top), n_x), (8, 3, all_rows, (top, INNER - top), n_x),
        (9, 2, all_rows, (top, INNER - top), n_x),
        (10, 7, (64, 64), (0, top), y_p), (11, 5, (0, 64), (0, top), y_m),
    ]
    lands = (4, 3, 1, 2, 2, 7, 5, 5, 7, 6, 6, 6)
    live = [n for n in range(12) if top < INNER or n not in (7, 8, 9)]

    def gather_send(*which):
        for n in which:
            if n in live:
                _, r, span, cols, device = gathers[n]
                gather(n, member(r), span, cols, device).start()

    def gather_wait(*which):
        for n in which:
            if n in live:
                _, _, span, cols, device = gathers[n]
                gather(n, member(lands[n]), span, cols, device).wait_recv()

    def exchange(n, h, r):
        src, dst = arrays[n]
        g = member(r)
        return remote(
            src.at[:, head_cols(g, h)], dst.at[h, own_rows, :], a2a_s.at[h, n, r], a2a_r.at[h, n, r], {"fsdp": g}
        )

    def give_back(n, h, r):
        src, dst = results[n]
        g = member(r)
        return remote(
            src.at[h, rows(g), :], dst.at[:, head_cols(f, h)], bk_s.at[h, n, r], bk_r.at[h, n, r], {"fsdp": g}
        )

    def keep_back(n, h):
        src, dst = results[n]
        return pltpu.make_async_copy(src.at[h, own_rows, :], dst.at[:, head_cols(f, h)], loc.at[4 + 2 * n + h])

    def swap_m(h):
        part = pl.ds(pl.multiple_of(h * 128, 128), 128)
        return remote(m16.at[part, :], mr.at[part, :], px_s.at[1 + h], px_r.at[1 + h], to_partner)

    for r in range(1, 8):
        remote(ids, idb.at[f], id_s.at[r], id_r.at[r], {"fsdp": member(r)}).start()
    gather_send(0, 1, 2)
    for n in range(3):
        for r in range(1, 8):
            exchange(n, 0, r).start()
    swap_p = remote(w16, pr, px_s.at[0], px_r.at[0], to_partner)
    swap_p.start()

    in_m.wait()
    in_id.wait()
    for r in range(1, 8):
        remote(ids, idb.at[back(r)], id_s.at[r], id_r.at[r], n_x).wait_recv()

    def stem_col(g, _):
        stem = lax.shift_right_logical(idb[g], 11).astype(F32)
        spread = jnp.broadcast_to(stem, (128, 128))
        skc[pl.ds(pl.multiple_of(g * 128, 128), 128), :] = spread.T
        return 0

    lax.fori_loop(0, 8, stem_col, 0)

    iota_k = lax.broadcasted_iota(jnp.int32, (128, 128), 0)
    iota_q = lax.broadcasted_iota(jnp.int32, (128, 128), 1)
    tri = jnp.where(iota_k <= iota_q, 0.0, NEG).astype(F32)

    def bias_row(kg, _):
        k_rows = pl.ds(pl.multiple_of(kg * 128, 128), 128)
        sk = skc[k_rows, :]
        bias[k_rows, k_rows] = tri

        def bias_tile(qg, _):
            sq = lax.shift_right_logical(idb[qg], 11).astype(F32)
            sq = sq + (1 - bm[qg, kg]).astype(F32) * 16.0
            bias[k_rows, pl.ds(pl.multiple_of(qg * 128, 128), 128)] = jnp.where(sk == sq, 0.0, NEG)
            return 0

        lax.fori_loop(kg + 1, 8, bias_tile, 0)
        return 0

    lax.fori_loop(0, 8, bias_row, 0)
    for ip in range(4):
        bias[256 * ip + 128 : 256 * ip + 256, 256 * ip : 256 * ip + 128] = jnp.full((128, 128), NEG, F32)

    inv_width = 1.0 / math.sqrt(INNER)
    scale = 1.0 / math.sqrt(HD)
    scale2 = scale * math.log2(math.e)

    def grad_block(block):
        at = rows(block)
        grad = (dot(ogb[at, :], w16[...], CT_MINOR) * inv_width).astype(BF)
        gr[0, at, :] = grad[:, :HD]
        gr[1, at, :] = grad[:, HD:]

    in_og.wait()
    grad_block(f)
    gather_wait(0, 1, 2)
    gather_send(3, 4, 5, 6, 7, 8)
    for r in range(1, 8):
        exchange(0, 1, r).start()
    for r in (4, 1, 3):
        grad_block(member(r))

    def forward(h, ip):
        size = 256 * (ip + 1)
        here = slice(256 * ip, 256 * ip + 256)
        s = dot(kb[h, 0:size, :], qb[h, here, :], CT_MINOR) * scale2 + bias[0:size, here]
        e = jnp.exp2(s - jnp.max(s, axis=0, keepdims=True))
        p = (e * (1.0 / jnp.sum(e, axis=0, keepdims=True))).astype(BF)
        pt[0:size, here] = p
        att[h, :, here] = dot(vb[h, 0:size, :], p, CT_MAJOR).astype(BF)

    def backward(h, ip):
        size = 256 * (ip + 1)
        here = slice(256 * ip, 256 * ip + 256)
        g = gr[h, here, :]
        p16 = pt[0:size, here]
        p = p16.astype(F32)
        dp = dot(vb[h, 0:size, :], g, CT_MINOR)
        row_dot = jnp.sum(p * dp, axis=0, keepdims=True)
        ds = (p * (dp - row_dot) * scale).astype(BF)
        dv_part = dot(p16, g, CT_PLAIN)
        dk_part = dot(ds, qb[h, here, :], CT_PLAIN)
        if ip == 3:
            dva[0:size, :] = dv_part
            dka[0:size, :] = dk_part
        else:
            dva[0:size, :] += dv_part
            dka[0:size, :] += dk_part
        dqb[h, here, :] = dot(ds, kb[h, 0:size, :], CT_MAJOR).astype(BF)

    def one_head(h, _):
        for n in range(3):
            in_head(n, h).wait()
            for r in range(1, 8):
                land = arrays[n][1].at[h, rows(back(r)), :]
                remote(land, land, a2a_s.at[h, n, r], a2a_r.at[h, n, r], n_x).wait_recv()
        for ip in range(4):
            forward(h, ip)

        @pl.when(h == 0)
        def _():
            gather_wait(3, 4, 5, 6)
            gather_send(9, 10, 11)
            for n in (1, 2):
                for r in range(1, 8):
                    exchange(n, 1, r).start()
            grad_block(member(2))
            gather_wait(7, 8)
            grad_block(member(5))
            grad_block(member(7))
            gather_wait(9, 10, 11)
            grad_block(member(6))

        h_rows = pl.ds(pl.multiple_of(h * 128, 128), 128)

        def weight_cols(n, _):
            cols = pl.ds(pl.multiple_of(n * 256, 256), 256)
            moment = MOMENTUM_RATE * mf[h_rows, cols] + dot(att[h], ogb[:, cols], CT_PLAIN) * inv_width
            mf[h_rows, cols] = moment
            m16[h_rows, cols] = moment.astype(BF)
            return 0

        lax.fori_loop(0, 8, weight_cols, 0)
        swap_m(h).start()
        for ip in (3, 2, 1, 0):
            backward(h, ip)

        def finish(n, _):
            part = pl.ds(pl.multiple_of(n * 128, 128), 128)
            dkb[h, part, :] = dka[part, :].astype(BF)
            dvb[h, part, :] = dva[part, :].astype(BF)
            return 0

        lax.fori_loop(0, 8, finish, 0)
        for n in range(3):
            for r in range(1, 8):
                give_back(n, h, r).start()
            keep_back(n, h).start()
        return 0

    lax.fori_loop(0, 2, one_head, 0)

    for r in range(1, 8):
        remote(ids, idb.at[f], id_s.at[r], id_r.at[r], n_x).wait_send()
    for n in live:
        _, r, span, cols, device = gathers[n]
        gather(n, member(r), span, cols, device).wait_send()

    def drain(h, _):
        for n in range(3):
            for r in range(1, 8):
                exchange(n, h, r).wait_send()
                give_back(n, h, r).wait_send()
                land = results[n][1].at[:, head_cols(back(r), h)]
                remote(land, land, bk_s.at[h, n, r], bk_r.at[h, n, r], n_x).wait_recv()
            keep_back(n, h).wait()
        swap_m(h).wait()
        return 0

    lax.fori_loop(0, 2, drain, 0)
    swap_p.wait()


def fused(bit, bm, q, k, v, og, params, mom, ids):
    anyspace = pl.BlockSpec(memory_space=pl.ANY)
    vmem = pl.BlockSpec(memory_space=pltpu.VMEM)
    tok = jax.ShapeDtypeStruct((128, INNER), BF)
    full = jax.ShapeDtypeStruct((256, INNER), F32)
    half = jax.ShapeDtypeStruct((256, INNER), BF)
    dma = pltpu.SemaphoreType.DMA
    heads = pltpu.VMEM((2, 1024, 128), BF)
    return pl.pallas_call(
        functools.partial(kernel, bit, INNER if bit == 1 else 1152),
        name=f"step_{bit}",
        out_shape=(tok, tok, tok, full, full, half, half),
        in_specs=[pl.BlockSpec(memory_space=pltpu.SMEM)] + [anyspace] * 7,
        out_specs=(vmem,) * 7,
        scratch_shapes=[
            heads, heads, heads,
            pltpu.VMEM((1024, INNER), BF),
            pltpu.VMEM((256, INNER), BF),
            pltpu.VMEM((256, INNER), BF),
            pltpu.VMEM((8, 1, 128), jnp.int32),
            pltpu.VMEM((1024, 128), F32),
            pltpu.VMEM((1024, 1024), F32),
            pltpu.VMEM((1024, 1024), BF),
            pltpu.VMEM((2, 128, 1024), BF),
            heads, heads, heads, heads,
            pltpu.VMEM((1024, 128), F32),
            pltpu.VMEM((1024, 128), F32),
            dma((12,)), dma((12,)), dma((2, 3, 8)), dma((2, 3, 8)), dma((8,)), dma((8,)),
            dma((2, 3, 8)), dma((2, 3, 8)), dma((3,)), dma((3,)), dma((10,)),
        ],
        compiler_params=pltpu.CompilerParams(
            collective_id=bit, has_side_effects=True, vmem_limit_bytes=46 * 1024 * 1024
        ),
    )(bm, q, k, v, og, params, mom, ids)


def finish_kernel(step, dq, dk, dv, pf, mf, pr, mr, o_dq, o_dk, o_dv, o_p, o_m, np_b, nm_b, sem, chunk_sem):
    copies = [pltpu.make_async_copy(a, b, sem.at[n]) for n, (a, b) in enumerate(((dq, o_dq), (dk, o_dk), (dv, o_dv)))]
    for copy in copies:
        copy.start()
    power = jnp.exp((jnp.zeros((8, 128), jnp.int32) + (step[0] + 1)).astype(F32) * math.log(MOMENTUM_RATE))
    rate = (LEARN_RATE * (1.0 / (1.0 - power)))[0:1, 0:1]
    for n in range(8):
        part = pl.ds(n * 32, 32)
        momentum = 0.5 * (mf[part, :] + mr[part, :].astype(F32))
        nm_b[part, :] = momentum
        np_b[part, :] = 0.5 * (pf[part, :] + pr[part, :].astype(F32)) - rate * momentum
        for m, (src, dst) in enumerate(((nm_b, o_m), (np_b, o_p))):
            copy = pltpu.make_async_copy(src.at[part, :], dst.at[part, :], chunk_sem.at[m, n])
            copy.start()
            copies.append(copy)
    for copy in copies:
        copy.wait()


def finish_call(step_index, *parts):
    anyspace = pl.BlockSpec(memory_space=pl.ANY)
    vmem = pl.BlockSpec(memory_space=pltpu.VMEM)
    tok = jax.ShapeDtypeStruct((128, INNER), BF)
    full = jax.ShapeDtypeStruct((256, INNER), F32)
    return pl.pallas_call(
        finish_kernel,
        name="finish",
        out_shape=(tok, tok, tok, full, full),
        in_specs=[pl.BlockSpec(memory_space=pltpu.SMEM)] + [vmem] * 7,
        out_specs=(anyspace,) * 5,
        scratch_shapes=[
            pltpu.VMEM((256, INNER), F32),
            pltpu.VMEM((256, INNER), F32),
            pltpu.SemaphoreType.DMA((3,)),
            pltpu.SemaphoreType.DMA((2, 8)),
        ],
        compiler_params=pltpu.CompilerParams(vmem_limit_bytes=16 * 1024 * 1024),
    )(step_index, *parts)


def shards(q, k, v, og, params, mom, token_ids, block_mask, step_index):
    ids = token_ids.reshape(1, 128)


    def branch(bit):
        def run(step, *parts):
            return finish_call(step, *fused(bit, *parts))

        return run

    return lax.switch(
        step_index[0] & 3,
        [branch(bit) for bit in range(4)],
        step_index, block_mask, q, k, v, og, params, mom, ids,
    )


def solution(mesh):
    split = P(("dp", "fsdp"), None)
    return jax.shard_map(
        shards,
        mesh=mesh,
        in_specs=(split,) * 6 + (P(("dp", "fsdp")), P(), P()),
        out_specs=(split,) * 5,
        check_vma=False,
    )
```

```python
import functools
import math

import jax
import jax.numpy as jnp
from jax import lax
from jax.experimental import pallas as pl
from jax.experimental.pallas import tpu as pltpu
from jax.sharding import PartitionSpec as P

HD = 128
INNER = 2048
MOMENTUM_RATE = 0.9
LEARN_RATE = 0.25
MESH = pl.DeviceIdType.MESH
NEG = -1e30
BF = jnp.bfloat16
F32 = jnp.float32
CT_MINOR = (((1,), (1,)), ((), ()))
CT_MAJOR = (((0,), (0,)), ((), ()))
CT_PLAIN = (((1,), (0,)), ((), ()))


def dot(a, b, dims):
    return lax.dot_general(a, b, dims, preferred_element_type=F32)


def kernel(
    bit, top,
    step_in, bm_in, q, k, v, og, params, mom, ids,
    dq, dk, dv, pf, mf,
    step, bm, pr, mr, qb, kb, vb, ogb, w16, m16, idb, skc, bias, pt, att, gr, dqb, dkb, dvb, dka, dva,
    ag_s, ag_r, a2a_s, a2a_r, id_s, id_r, bk_s, bk_r, px_s, px_r, loc,
):
    f = lax.axis_index("fsdp")
    d = lax.axis_index("dp")
    x = f // 4
    y = lax.rem(f, 4)

    def member(r):
        return lax.rem(x + r // 4, 2) * 4 + lax.rem(y + r % 4, 4)

    def back(r):
        return lax.rem(x + r // 4, 2) * 4 + lax.rem(y + 4 - r % 4, 4)

    width = 1 << bit
    partner = d + width - 2 * width * lax.rem(d // width, 2)
    to_partner = {"dp": partner}

    def rows(block, start=0, size=128):
        return pl.ds(pl.multiple_of(block * 128 + start, 16), size)

    def head_cols(block, h):
        return pl.ds(pl.multiple_of(block * 256 + h * 128, 128), 128)

    def remote(src, dst, s_sem, r_sem, device):
        return pltpu.make_async_remote_copy(
            src_ref=src, dst_ref=dst, send_sem=s_sem, recv_sem=r_sem, device_id=device, device_id_type=MESH
        )

    own_rows = rows(f)
    arrays = ((q, qb), (k, kb), (v, vb))
    results = ((dqb, dq), (dkb, dk), (dvb, dv))
    quarters = [pl.ds(64 * n, 64) for n in range(4)]
    in_p = [pltpu.make_async_copy(params.at[part, :], pf.at[part, :], loc.at[10 + n]) for n, part in enumerate(quarters)]
    in_bm = pltpu.make_async_copy(bm_in, bm, loc.at[14])
    in_step = pltpu.make_async_copy(step_in, step, loc.at[0])
    in_m = pltpu.make_async_copy(mom, mf, loc.at[1])
    in_id = pltpu.make_async_copy(ids, idb.at[f], loc.at[2])
    in_og = pltpu.make_async_copy(og, ogb.at[own_rows, :], loc.at[3])

    def in_head(n, h):
        src, dst = arrays[n]
        return pltpu.make_async_copy(src.at[:, head_cols(f, h)], dst.at[h, own_rows, :], loc.at[4 + 2 * n + h])

    barrier = pltpu.get_barrier_semaphore()
    for r in range(1, 8):
        pl.semaphore_signal(barrier, inc=1, device_id={"fsdp": member(r)}, device_id_type=MESH)
    pl.semaphore_signal(barrier, inc=1, device_id=to_partner, device_id_type=MESH)
    for copy in (*in_p, in_id, in_bm, in_og, in_m, in_step):
        copy.start()
    for n in range(3):
        for h in range(2):
            in_head(n, h).start()

    pl.semaphore_wait(barrier, 8)

    n_x = {"fsdp": member(4)}
    y_p = {"fsdp": member(1)}
    y_m = {"fsdp": member(3)}
    all_rows = (0, 128)
    all_cols = (0, INNER)

    def gather(n, block, span, cols, device):
        part = ogb.at[rows(block, *span), pl.ds(cols[0], cols[1])]
        return remote(og if n < 3 else part, part, ag_s.at[n], ag_r.at[n], device)

    gathers = [
        (0, 0, all_rows, all_cols, n_x), (1, 0, all_rows, all_cols, y_p), (2, 0, all_rows, all_cols, y_m),
        (3, 1, (0, 64), all_cols, y_m), (4, 3, (64, 64), all_cols, y_p),
        (5, 4, all_rows, (0, top), y_p), (6, 4, all_rows, (0, top), y_m),
        (7, 1, all_rows, (top, INNER - top), n_x), (8, 3, all_rows, (top, INNER - top), n_x),
        (9, 2, all_rows, (top, INNER - top), n_x),
        (10, 7, (64, 64), (0, top), y_p), (11, 5, (0, 64), (0, top), y_m),
    ]
    lands = (4, 3, 1, 2, 2, 7, 5, 5, 7, 6, 6, 6)
    live = [n for n in range(12) if top < INNER or n not in (7, 8, 9)]

    def gather_send(*which):
        for n in which:
            if n in live:
                _, r, span, cols, device = gathers[n]
                gather(n, member(r), span, cols, device).start()

    def gather_wait(*which):
        for n in which:
            if n in live:
                _, _, span, cols, device = gathers[n]
                gather(n, member(lands[n]), span, cols, device).wait_recv()

    def exchange(n, h, r):
        src, dst = arrays[n]
        g = member(r)
        return remote(
            src.at[:, head_cols(g, h)], dst.at[h, own_rows, :], a2a_s.at[h, n, r], a2a_r.at[h, n, r], {"fsdp": g}
        )

    def give_back(n, h, r):
        src, dst = results[n]
        g = member(r)
        return remote(
            src.at[h, rows(g), :], dst.at[:, head_cols(f, h)], bk_s.at[h, n, r], bk_r.at[h, n, r], {"fsdp": g}
        )

    def keep_back(n, h):
        src, dst = results[n]
        return pltpu.make_async_copy(src.at[h, own_rows, :], dst.at[:, head_cols(f, h)], loc.at[4 + 2 * n + h])

    def swap_m(h, n):
        part = (pl.ds(pl.multiple_of(h * 128, 128), 128), pl.ds(pl.multiple_of(n * 256, 256), 256))
        return remote(m16.at[part], mr.at[part], px_s.at[1 + h * 8 + n], px_r.at[1 + h * 8 + n], to_partner)

    for r in range(1, 8):
        remote(ids, idb.at[f], id_s.at[r], id_r.at[r], {"fsdp": member(r)}).start()
    gather_send(0, 1, 2)

    def exchange_first():
        for n in range(3):
            for r in range(1, 8):
                exchange(n, 0, r).start()

    def swap_p(n):
        part = quarters[n]
        return remote(w16.at[part, :], pr.at[part, :], px_s.at[17 + n], px_r.at[17 + n], to_partner)

    if bit == 1:
        exchange_first()
    for n, part in enumerate(quarters):
        in_p[n].wait()
        w16[part, :] = pf[part, :].astype(BF)
        if n:
            swap_p(n - 1).start()
    if bit != 1:
        exchange_first()
    swap_p(3).start()
    in_m.wait()
    in_id.wait()
    in_bm.wait()
    in_step.wait()
    for r in range(1, 8):
        remote(ids, idb.at[back(r)], id_s.at[r], id_r.at[r], n_x).wait_recv()

    def stem_col(g, _):
        stem = lax.shift_right_logical(idb[g], 11).astype(F32)
        spread = jnp.broadcast_to(stem, (128, 128))
        skc[pl.ds(pl.multiple_of(g * 128, 128), 128), :] = spread.T
        return 0

    lax.fori_loop(0, 8, stem_col, 0)

    iota_k = lax.broadcasted_iota(jnp.int32, (128, 128), 0)
    iota_q = lax.broadcasted_iota(jnp.int32, (128, 128), 1)
    tri = jnp.where(iota_k <= iota_q, 0.0, NEG).astype(F32)

    def bias_row(kg, _):
        k_rows = pl.ds(pl.multiple_of(kg * 128, 128), 128)
        sk = skc[k_rows, :]
        bias[k_rows, k_rows] = tri

        def bias_tile(qg, _):
            sq = lax.shift_right_logical(idb[qg], 11).astype(F32)
            sq = sq + (1 - bm[qg, kg]).astype(F32) * 16.0
            bias[k_rows, pl.ds(pl.multiple_of(qg * 128, 128), 128)] = jnp.where(sk == sq, 0.0, NEG)
            return 0

        lax.fori_loop(kg + 1, 8, bias_tile, 0)
        return 0

    lax.fori_loop(0, 8, bias_row, 0)
    for ip in range(4):
        bias[256 * ip + 128 : 256 * ip + 256, 256 * ip : 256 * ip + 128] = jnp.full((128, 128), NEG, F32)

    inv_width = 1.0 / math.sqrt(INNER)
    scale = 1.0 / math.sqrt(HD)
    scale2 = scale * math.log2(math.e)

    def grad_block(block):
        at = rows(block)
        grad = (dot(ogb[at, :], w16[...], CT_MINOR) * inv_width).astype(BF)
        gr[0, at, :] = grad[:, :HD]
        gr[1, at, :] = grad[:, HD:]

    in_og.wait()
    grad_block(f)
    gather_wait(0, 1, 2)
    gather_send(3, 4, 5, 6, 7, 8)
    for r in (4, 1, 3):
        grad_block(member(r))

    def forward(h, ip):
        size = 256 * (ip + 1)
        here = slice(256 * ip, 256 * ip + 256)
        s = dot(kb[h, 0:size, :], qb[h, here, :], CT_MINOR) * scale2 + bias[0:size, here]
        e = jnp.exp2(s - jnp.max(s, axis=0, keepdims=True))
        p = (e * (1.0 / jnp.sum(e, axis=0, keepdims=True))).astype(BF)
        pt[0:size, here] = p
        att[h, :, here] = dot(vb[h, 0:size, :], p, CT_MAJOR).astype(BF)

    def backward(h, ip):
        size = 256 * (ip + 1)
        here = slice(256 * ip, 256 * ip + 256)
        g = gr[h, here, :]
        p16 = pt[0:size, here]
        p = p16.astype(F32)
        dp = dot(vb[h, 0:size, :], g, CT_MINOR)
        row_dot = jnp.sum(p * dp, axis=0, keepdims=True)
        ds = (p * (dp - row_dot) * scale).astype(BF)
        dv_part = dot(p16, g, CT_PLAIN)
        dk_part = dot(ds, qb[h, here, :], CT_PLAIN)
        if ip == 3:
            dva[0:size, :] = dv_part
            dka[0:size, :] = dk_part
        else:
            dva[0:size, :] += dv_part
            dka[0:size, :] += dk_part
        dqb[h, here, :] = dot(ds, kb[h, 0:size, :], CT_MAJOR).astype(BF)

    def one_head(h, _):
        for n in range(3):
            in_head(n, h).wait()
            for r in range(1, 8):
                land = arrays[n][1].at[h, rows(back(r)), :]
                remote(land, land, a2a_s.at[h, n, r], a2a_r.at[h, n, r], n_x).wait_recv()
        for ip in range(4):
            forward(h, ip)

        @pl.when(h == 0)
        def _():
            gather_wait(3, 4)
            gather_send(9)
            for r in (1, 2, 3):
                exchange(0, 1, r).start()
            grad_block(member(2))
            gather_wait(5, 6)
            gather_send(10, 11)
            for n in range(3):
                for r in range(4 if n == 0 else 1, 8):
                    exchange(n, 1, r).start()
            gather_wait(7, 8)
            grad_block(member(5))
            grad_block(member(7))
            gather_wait(9, 10, 11)
            grad_block(member(6))

        def weight():
            h_rows = pl.ds(pl.multiple_of(h * 128, 128), 128)

            def weight_cols(n, _):
                cols = pl.ds(pl.multiple_of(n * 256, 256), 256)
                moment = MOMENTUM_RATE * mf[h_rows, cols] + dot(att[h], ogb[:, cols], CT_PLAIN) * inv_width
                mf[h_rows, cols] = moment
                m16[h_rows, cols] = moment.astype(BF)

                @pl.when(n > 0)
                def _():
                    swap_m(h, n - 1).start()

                return 0

            lax.fori_loop(0, 8, weight_cols, 0)
            swap_m(h, 7).start()

        def finish(n, _):
            part = pl.ds(pl.multiple_of(n * 128, 128), 128)
            dkb[h, part, :] = dka[part, :].astype(BF)
            dvb[h, part, :] = dva[part, :].astype(BF)
            return 0

        if bit in (1, 2):
            weight()
        for ip in (3, 2, 1, 0):
            backward(h, ip)
        lax.fori_loop(0, 8, finish, 0)
        for n in range(3):
            for r in range(1, 8):
                give_back(n, h, r).start()
            keep_back(n, h).start()
        if bit in (0, 3):
            weight()
        return 0

    lax.fori_loop(0, 2, one_head, 0)

    for r in range(1, 8):
        remote(ids, idb.at[f], id_s.at[r], id_r.at[r], n_x).wait_send()
    for n in live:
        _, r, span, cols, device = gathers[n]
        gather(n, member(r), span, cols, device).wait_send()

    def drain_back(h):
        for n in range(3):
            for r in range(1, 8):
                exchange(n, h, r).wait_send()
                give_back(n, h, r).wait_send()
                land = results[n][1].at[:, head_cols(back(r), h)]
                remote(land, land, bk_s.at[h, n, r], bk_r.at[h, n, r], n_x).wait_recv()
            keep_back(n, h).wait()

    power = jnp.exp((jnp.zeros((8, 128), jnp.int32) + (step[0] + 1)).astype(F32) * math.log(MOMENTUM_RATE))
    rate = (LEARN_RATE * (1.0 / (1.0 - power)))[0:1, 0:1]

    def drain_m(h):
        for n in range(8):
            swap_m(h, n).wait()

        def average(n, _):
            part = pl.ds(pl.multiple_of(h * 128 + n * 16, 16), 16)
            momentum = 0.5 * (mf[part, :] + mr[part, :].astype(F32))
            mf[part, :] = momentum
            pf[part, :] = 0.5 * (pf[part, :] + pr[part, :].astype(F32)) - rate * momentum
            return 0

        lax.fori_loop(0, 8, average, 0)

    for n in range(4):
        swap_p(n).wait()
    drain_m(0)
    drain_back(0)
    if bit == 0:
        drain_m(1)
    drain_back(1)
    if bit != 0:
        drain_m(1)


def fused(bit, step, bm, q, k, v, og, params, mom, ids):
    anyspace = pl.BlockSpec(memory_space=pl.ANY)
    vmem = pl.BlockSpec(memory_space=pltpu.VMEM)
    tok = jax.ShapeDtypeStruct((128, INNER), BF)
    full = jax.ShapeDtypeStruct((256, INNER), F32)
    half = pltpu.VMEM((256, INNER), BF)
    dma = pltpu.SemaphoreType.DMA
    heads = pltpu.VMEM((2, 1024, 128), BF)
    return pl.pallas_call(
        functools.partial(kernel, bit, INNER if bit == 1 else 1152),
        name=f"step_{bit}",
        out_shape=(tok, tok, tok, full, full),
        in_specs=[anyspace] * 9,
        out_specs=(vmem,) * 5,
        scratch_shapes=[
            pltpu.SMEM((1,), jnp.int32),
            pltpu.SMEM((8, 8), jnp.int32),
            half, half,
            heads, heads, heads,
            pltpu.VMEM((1024, INNER), BF),
            pltpu.VMEM((256, INNER), BF),
            pltpu.VMEM((256, INNER), BF),
            pltpu.VMEM((8, 1, 128), jnp.int32),
            pltpu.VMEM((1024, 128), F32),
            pltpu.VMEM((1024, 1024), F32),
            pltpu.VMEM((1024, 1024), BF),
            pltpu.VMEM((2, 128, 1024), BF),
            heads, heads, heads, heads,
            pltpu.VMEM((1024, 128), F32),
            pltpu.VMEM((1024, 128), F32),
            dma((12,)), dma((12,)), dma((2, 3, 8)), dma((2, 3, 8)), dma((8,)), dma((8,)),
            dma((2, 3, 8)), dma((2, 3, 8)), dma((21,)), dma((21,)), dma((15,)),
        ],
        compiler_params=pltpu.CompilerParams(
            collective_id=bit, has_side_effects=True, vmem_limit_bytes=46 * 1024 * 1024
        ),
    )(step, bm, q, k, v, og, params, mom, ids)


def finish_kernel(*refs):
    copies = []
    for n in range(5):
        src, dst = refs[n], refs[5 + n]
        size = src.shape[0] // 2
        for m in range(2):
            part = pl.ds(m * size, size)
            copies.append(pltpu.make_async_copy(src.at[part, :], dst.at[part, :], refs[10].at[n, m]))
            copies[-1].start()
    for copy in copies:
        copy.wait()


def finish_call(*parts):
    anyspace = pl.BlockSpec(memory_space=pl.ANY)
    vmem = pl.BlockSpec(memory_space=pltpu.VMEM)
    return pl.pallas_call(
        finish_kernel,
        name="finish",
        out_shape=tuple(jax.ShapeDtypeStruct(part.shape, part.dtype) for part in parts),
        in_specs=[vmem] * 5,
        out_specs=(anyspace,) * 5,
        scratch_shapes=[pltpu.SemaphoreType.DMA((5, 2))],
        compiler_params=pltpu.CompilerParams(vmem_limit_bytes=16 * 1024 * 1024),
    )(*parts)


def shards(q, k, v, og, params, mom, token_ids, block_mask, step_index):
    ids = token_ids.reshape(1, 128)


    def branch(bit):
        def run(*parts):
            return finish_call(*fused(bit, *parts))

        return run

    return lax.switch(
        step_index[0] & 3,
        [branch(bit) for bit in range(4)],
        step_index, block_mask, q, k, v, og, params, mom, ids,
    )


def solution(mesh):
    split = P(("dp", "fsdp"), None)
    return jax.shard_map(
        shards,
        mesh=mesh,
        in_specs=(split,) * 6 + (P(("dp", "fsdp")), P(), P()),
        out_specs=(split,) * 5,
        check_vma=False,
    )
```

```python
import functools
import math

import jax
import jax.numpy as jnp
from jax import lax
from jax.experimental import pallas as pl
from jax.experimental.pallas import tpu as pltpu
from jax.sharding import PartitionSpec as P

HD = 128
INNER = 2048
MOMENTUM_RATE = 0.9
LEARN_RATE = 0.25
MESH = pl.DeviceIdType.MESH
NEG = -1e30
BF = jnp.bfloat16
F32 = jnp.float32
CT_MINOR = (((1,), (1,)), ((), ()))
CT_MAJOR = (((0,), (0,)), ((), ()))
CT_PLAIN = (((1,), (0,)), ((), ()))


def dot(a, b, dims):
    return lax.dot_general(a, b, dims, preferred_element_type=F32)


def kernel(
    bit, top,
    step_in, bm_in, q, k, v, og, params, mom, ids,
    dq, dk, dv, pf, mf,
    step, bm, pr, mr, qb, kb, vb, ogb, w16, m16, idb, skc, bias, pt, att, gr, dqb, dkb, dvb, dka, dva,
    ag_s, ag_r, a2a_s, a2a_r, id_s, id_r, bk_s, bk_r, px_s, px_r, loc,
):
    f = lax.axis_index("fsdp")
    d = lax.axis_index("dp")
    x = f // 4
    y = lax.rem(f, 4)

    def member(r):
        return lax.rem(x + r // 4, 2) * 4 + lax.rem(y + r % 4, 4)

    def back(r):
        return lax.rem(x + r // 4, 2) * 4 + lax.rem(y + 4 - r % 4, 4)

    width = 1 << bit
    partner = d + width - 2 * width * lax.rem(d // width, 2)
    to_partner = {"dp": partner}

    def rows(block, start=0, size=128):
        return pl.ds(pl.multiple_of(block * 128 + start, 16), size)

    def head_cols(block, h):
        return pl.ds(pl.multiple_of(block * 256 + h * 128, 128), 128)

    def remote(src, dst, s_sem, r_sem, device):
        return pltpu.make_async_remote_copy(
            src_ref=src, dst_ref=dst, send_sem=s_sem, recv_sem=r_sem, device_id=device, device_id_type=MESH
        )

    own_rows = rows(f)
    arrays = ((q, qb), (k, kb), (v, vb))
    results = ((dqb, dq), (dkb, dk), (dvb, dv))
    quarters = [pl.ds(64 * n, 64) for n in range(4)]
    in_p = [pltpu.make_async_copy(params.at[part, :], pf.at[part, :], loc.at[10 + n]) for n, part in enumerate(quarters)]
    in_bm = pltpu.make_async_copy(bm_in, bm, loc.at[14])
    in_step = pltpu.make_async_copy(step_in, step, loc.at[0])
    in_m = pltpu.make_async_copy(mom, mf, loc.at[1])
    in_id = pltpu.make_async_copy(ids, idb.at[f], loc.at[2])
    in_og = pltpu.make_async_copy(og, ogb.at[own_rows, :], loc.at[3])

    def in_head(n, h):
        src, dst = arrays[n]
        return pltpu.make_async_copy(src.at[:, head_cols(f, h)], dst.at[h, own_rows, :], loc.at[4 + 2 * n + h])

    barrier = pltpu.get_barrier_semaphore()
    for r in range(1, 8):
        pl.semaphore_signal(barrier, inc=1, device_id={"fsdp": member(r)}, device_id_type=MESH)
    pl.semaphore_signal(barrier, inc=1, device_id=to_partner, device_id_type=MESH)
    for copy in (*in_p, in_id, in_bm, in_og, in_m, in_step):
        copy.start()
    for n in range(3):
        for h in range(2):
            in_head(n, h).start()

    pl.semaphore_wait(barrier, 8)

    n_x = {"fsdp": member(4)}
    y_p = {"fsdp": member(1)}
    y_m = {"fsdp": member(3)}
    all_rows = (0, 128)
    all_cols = (0, INNER)

    def gather(n, block, span, cols, device):
        part = ogb.at[rows(block, *span), pl.ds(cols[0], cols[1])]
        return remote(og if n < 3 else part, part, ag_s.at[n], ag_r.at[n], device)

    gathers = [
        (0, 0, all_rows, all_cols, n_x), (1, 0, all_rows, all_cols, y_p), (2, 0, all_rows, all_cols, y_m),
        (3, 1, (0, 64), all_cols, y_m), (4, 3, (64, 64), all_cols, y_p),
        (5, 4, all_rows, (0, top), y_p), (6, 4, all_rows, (0, top), y_m),
        (7, 1, all_rows, (top, INNER - top), n_x), (8, 3, all_rows, (top, INNER - top), n_x),
        (9, 2, all_rows, (top, INNER - top), n_x),
        (10, 7, (64, 64), (0, top), y_p), (11, 5, (0, 64), (0, top), y_m),
    ]
    lands = (4, 3, 1, 2, 2, 7, 5, 5, 7, 6, 6, 6)
    live = [n for n in range(12) if top < INNER or n not in (7, 8, 9)]

    def gather_send(*which):
        for n in which:
            if n in live:
                _, r, span, cols, device = gathers[n]
                gather(n, member(r), span, cols, device).start()

    def gather_wait(*which):
        for n in which:
            if n in live:
                _, _, span, cols, device = gathers[n]
                gather(n, member(lands[n]), span, cols, device).wait_recv()

    def exchange(n, h, r):
        src, dst = arrays[n]
        g = member(r)
        return remote(
            src.at[:, head_cols(g, h)], dst.at[h, own_rows, :], a2a_s.at[h, n, r], a2a_r.at[h, n, r], {"fsdp": g}
        )

    def give_back(n, h, r):
        src, dst = results[n]
        g = member(r)
        return remote(
            src.at[h, rows(g), :], dst.at[:, head_cols(f, h)], bk_s.at[h, n, r], bk_r.at[h, n, r], {"fsdp": g}
        )

    def keep_back(n, h):
        src, dst = results[n]
        return pltpu.make_async_copy(src.at[h, own_rows, :], dst.at[:, head_cols(f, h)], loc.at[4 + 2 * n + h])

    def swap_m(h, n):
        part = (pl.ds(pl.multiple_of(h * 128, 128), 128), pl.ds(pl.multiple_of(n * 256, 256), 256))
        return remote(m16.at[part], mr.at[part], px_s.at[1 + h * 8 + n], px_r.at[1 + h * 8 + n], to_partner)

    for r in range(1, 8):
        remote(ids, idb.at[f], id_s.at[r], id_r.at[r], {"fsdp": member(r)}).start()
    gather_send(0, 1, 2)

    def exchange_first():
        for n in range(3):
            for r in range(1, 8):
                exchange(n, 0, r).start()

    def swap_p(n):
        part = quarters[n]
        return remote(w16.at[part, :], pr.at[part, :], px_s.at[17 + n], px_r.at[17 + n], to_partner)

    if bit == 1:
        exchange_first()
    for n, part in enumerate(quarters):
        in_p[n].wait()
        w16[part, :] = pf[part, :].astype(BF)
        if n:
            swap_p(n - 1).start()
    if bit != 1:
        exchange_first()
    swap_p(3).start()
    in_m.wait()
    in_id.wait()
    in_bm.wait()
    in_step.wait()
    for r in range(1, 8):
        remote(ids, idb.at[back(r)], id_s.at[r], id_r.at[r], n_x).wait_recv()

    def stem_col(g, _):
        stem = lax.shift_right_logical(idb[g], 11).astype(F32)
        spread = jnp.broadcast_to(stem, (128, 128))
        skc[pl.ds(pl.multiple_of(g * 128, 128), 128), :] = spread.T
        return 0

    lax.fori_loop(0, 8, stem_col, 0)

    iota_k = lax.broadcasted_iota(jnp.int32, (128, 128), 0)
    iota_q = lax.broadcasted_iota(jnp.int32, (128, 128), 1)
    tri = jnp.where(iota_k <= iota_q, 0.0, NEG).astype(F32)

    def bias_row(kg, _):
        k_rows = pl.ds(pl.multiple_of(kg * 128, 128), 128)
        sk = skc[k_rows, :]
        bias[k_rows, k_rows] = tri

        def bias_tile(qg, _):
            sq = lax.shift_right_logical(idb[qg], 11).astype(F32)
            sq = sq + (1 - bm[qg, kg]).astype(F32) * 16.0
            bias[k_rows, pl.ds(pl.multiple_of(qg * 128, 128), 128)] = jnp.where(sk == sq, 0.0, NEG)
            return 0

        lax.fori_loop(kg + 1, 8, bias_tile, 0)
        return 0

    lax.fori_loop(0, 8, bias_row, 0)
    for ip in range(4):
        bias[256 * ip + 128 : 256 * ip + 256, 256 * ip : 256 * ip + 128] = jnp.full((128, 128), NEG, F32)

    inv_width = 1.0 / math.sqrt(INNER)
    scale = 1.0 / math.sqrt(HD)
    scale2 = scale * math.log2(math.e)

    def grad_block(block):
        at = rows(block)
        grad = (dot(ogb[at, :], w16[...], CT_MINOR) * inv_width).astype(BF)
        gr[0, at, :] = grad[:, :HD]
        gr[1, at, :] = grad[:, HD:]

    in_og.wait()
    grad_block(f)
    gather_wait(0, 1, 2)
    gather_send(3, 4, 5, 6, 7, 8)
    for r in (4, 1, 3):
        grad_block(member(r))

    def forward(h, ip):
        size = 256 * (ip + 1)
        here = slice(256 * ip, 256 * ip + 256)
        s = dot(kb[h, 0:size, :], qb[h, here, :], CT_MINOR) * scale2 + bias[0:size, here]
        e = jnp.exp2(s - jnp.max(s, axis=0, keepdims=True))
        p = (e * (1.0 / jnp.sum(e, axis=0, keepdims=True))).astype(BF)
        pt[0:size, here] = p
        att[h, :, here] = dot(vb[h, 0:size, :], p, CT_MAJOR).astype(BF)

    def backward(h, ip):
        size = 256 * (ip + 1)
        here = slice(256 * ip, 256 * ip + 256)
        g = gr[h, here, :]
        p16 = pt[0:size, here]
        p = p16.astype(F32)
        dp = dot(vb[h, 0:size, :], g, CT_MINOR)
        row_dot = jnp.sum(p * dp, axis=0, keepdims=True)
        ds = (p * (dp - row_dot) * scale).astype(BF)
        dv_part = dot(p16, g, CT_PLAIN)
        dk_part = dot(ds, qb[h, here, :], CT_PLAIN)
        if ip == 3:
            dva[0:size, :] = dv_part
            dka[0:size, :] = dk_part
        else:
            dva[0:size, :] += dv_part
            dka[0:size, :] += dk_part
        dqb[h, here, :] = dot(ds, kb[h, 0:size, :], CT_MAJOR).astype(BF)

    def one_head(h, _):
        for n in range(3):
            in_head(n, h).wait()
            for r in range(1, 8):
                land = arrays[n][1].at[h, rows(back(r)), :]
                remote(land, land, a2a_s.at[h, n, r], a2a_r.at[h, n, r], n_x).wait_recv()
        for ip in range(4):
            forward(h, ip)

        @pl.when(h == 0)
        def _():
            gather_wait(3, 4)
            gather_send(9)
            for r in (1, 2, 3):
                exchange(0, 1, r).start()
            grad_block(member(2))
            gather_wait(5, 6)
            gather_send(10, 11)
            for n in range(3):
                for r in range(4 if n == 0 else 1, 8):
                    exchange(n, 1, r).start()
            gather_wait(7, 8)
            grad_block(member(5))
            grad_block(member(7))
            gather_wait(9, 10, 11)
            grad_block(member(6))

        def weight():
            h_rows = pl.ds(pl.multiple_of(h * 128, 128), 128)

            def weight_cols(n, _):
                cols = pl.ds(pl.multiple_of(n * 256, 256), 256)
                moment = MOMENTUM_RATE * mf[h_rows, cols] + dot(att[h], ogb[:, cols], CT_PLAIN) * inv_width
                mf[h_rows, cols] = moment
                m16[h_rows, cols] = moment.astype(BF)

                @pl.when(n > 0)
                def _():
                    swap_m(h, n - 1).start()

                return 0

            lax.fori_loop(0, 8, weight_cols, 0)
            swap_m(h, 7).start()

        def finish(n, _):
            part = pl.ds(pl.multiple_of(n * 128, 128), 128)
            dkb[h, part, :] = dka[part, :].astype(BF)
            dvb[h, part, :] = dva[part, :].astype(BF)
            return 0

        if bit in (1, 2):
            weight()
        for ip in (3, 2, 1, 0):
            backward(h, ip)
        lax.fori_loop(0, 8, finish, 0)
        for n in range(3):
            for r in range(1, 8):
                give_back(n, h, r).start()
            keep_back(n, h).start()
        if bit in (0, 3):
            weight()
        return 0

    lax.fori_loop(0, 2, one_head, 0)

    for r in range(1, 8):
        remote(ids, idb.at[f], id_s.at[r], id_r.at[r], n_x).wait_send()
    for n in live:
        _, r, span, cols, device = gathers[n]
        gather(n, member(r), span, cols, device).wait_send()

    def drain_back(h):
        for n in range(3):
            for r in range(1, 8):
                exchange(n, h, r).wait_send()
                give_back(n, h, r).wait_send()
                land = results[n][1].at[:, head_cols(back(r), h)]
                remote(land, land, bk_s.at[h, n, r], bk_r.at[h, n, r], n_x).wait_recv()
            keep_back(n, h).wait()

    power = jnp.exp((jnp.zeros((8, 128), jnp.int32) + (step[0] + 1)).astype(F32) * math.log(MOMENTUM_RATE))
    rate = (LEARN_RATE * (1.0 / (1.0 - power)))[0:1, 0:1]

    def drain_m(h):
        part = pl.ds(h * 128, 128)

        def average(n, _):
            swap_m(h, n).wait()
            cols = pl.ds(pl.multiple_of(n * 256, 256), 256)
            momentum = 0.5 * (mf[part, cols] + mr[part, cols].astype(F32))
            mf[part, cols] = momentum
            pf[part, cols] = 0.5 * (pf[part, cols] + pr[part, cols].astype(F32)) - rate * momentum
            return 0

        lax.fori_loop(0, 8, average, 0)

    for n in range(4):
        swap_p(n).wait()
    drain_m(0)
    drain_back(0)
    if bit == 0:
        drain_m(1)
    drain_back(1)
    if bit != 0:
        drain_m(1)


def fused(bit, step, bm, q, k, v, og, params, mom, ids):
    anyspace = pl.BlockSpec(memory_space=pl.ANY)
    vmem = pl.BlockSpec(memory_space=pltpu.VMEM)
    tok = jax.ShapeDtypeStruct((128, INNER), BF)
    full = jax.ShapeDtypeStruct((256, INNER), F32)
    half = pltpu.VMEM((256, INNER), BF)
    dma = pltpu.SemaphoreType.DMA
    heads = pltpu.VMEM((2, 1024, 128), BF)
    return pl.pallas_call(
        functools.partial(kernel, bit, INNER if bit == 1 else 1152),
        name=f"step_{bit}",
        out_shape=(tok, tok, tok, full, full),
        in_specs=[anyspace] * 9,
        out_specs=(vmem,) * 5,
        scratch_shapes=[
            pltpu.SMEM((1,), jnp.int32),
            pltpu.SMEM((8, 8), jnp.int32),
            half, half,
            heads, heads, heads,
            pltpu.VMEM((1024, INNER), BF),
            pltpu.VMEM((256, INNER), BF),
            pltpu.VMEM((256, INNER), BF),
            pltpu.VMEM((8, 1, 128), jnp.int32),
            pltpu.VMEM((1024, 128), F32),
            pltpu.VMEM((1024, 1024), F32),
            pltpu.VMEM((1024, 1024), BF),
            pltpu.VMEM((2, 128, 1024), BF),
            heads, heads, heads, heads,
            pltpu.VMEM((1024, 128), F32),
            pltpu.VMEM((1024, 128), F32),
            dma((12,)), dma((12,)), dma((2, 3, 8)), dma((2, 3, 8)), dma((8,)), dma((8,)),
            dma((2, 3, 8)), dma((2, 3, 8)), dma((21,)), dma((21,)), dma((15,)),
        ],
        compiler_params=pltpu.CompilerParams(
            collective_id=bit, has_side_effects=True, vmem_limit_bytes=46 * 1024 * 1024
        ),
    )(step, bm, q, k, v, og, params, mom, ids)


def finish_kernel(*refs):
    copies = []
    for n in range(5):
        src, dst = refs[n], refs[5 + n]
        size = src.shape[0] // 2
        for m in range(2):
            part = pl.ds(m * size, size)
            copies.append(pltpu.make_async_copy(src.at[part, :], dst.at[part, :], refs[10].at[n, m]))
            copies[-1].start()
    for copy in copies:
        copy.wait()


def finish_call(*parts):
    anyspace = pl.BlockSpec(memory_space=pl.ANY)
    vmem = pl.BlockSpec(memory_space=pltpu.VMEM)
    return pl.pallas_call(
        finish_kernel,
        name="finish",
        out_shape=tuple(jax.ShapeDtypeStruct(part.shape, part.dtype) for part in parts),
        in_specs=[vmem] * 5,
        out_specs=(anyspace,) * 5,
        scratch_shapes=[pltpu.SemaphoreType.DMA((5, 2))],
        compiler_params=pltpu.CompilerParams(vmem_limit_bytes=16 * 1024 * 1024),
    )(*parts)


def shards(q, k, v, og, params, mom, token_ids, block_mask, step_index):
    ids = token_ids.reshape(1, 128)


    def branch(bit):
        def run(*parts):
            return finish_call(*fused(bit, *parts))

        return run

    return lax.switch(
        step_index[0] & 3,
        [branch(bit) for bit in range(4)],
        step_index, block_mask, q, k, v, og, params, mom, ids,
    )


def solution(mesh):
    split = P(("dp", "fsdp"), None)
    return jax.shard_map(
        shards,
        mesh=mesh,
        in_specs=(split,) * 6 + (P(("dp", "fsdp")), P(), P()),
        out_specs=(split,) * 5,
        check_vma=False,
    )
```

```python
import functools
import math

import jax
import jax.numpy as jnp
from jax import lax
from jax.experimental import pallas as pl
from jax.experimental.pallas import tpu as pltpu
from jax.sharding import PartitionSpec as P

HD = 128
INNER = 2048
MOMENTUM_RATE = 0.9
LEARN_RATE = 0.25
MESH = pl.DeviceIdType.MESH
NEG = -1e30
BF = jnp.bfloat16
F32 = jnp.float32
CT_MINOR = (((1,), (1,)), ((), ()))
CT_MAJOR = (((0,), (0,)), ((), ()))
CT_PLAIN = (((1,), (0,)), ((), ()))


def dot(a, b, dims):
    return lax.dot_general(a, b, dims, preferred_element_type=F32)


def kernel(
    bit, top,
    step_in, bm_in, q, k, v, og, params, mom, ids,
    dq, dk, dv, pf, mf,
    step, bm, pr, mr, qb, kb, vb, ogb, w16, m16, idb, skc, bias, pt, att, gr, dqb, dkb, dvb, dka, dva,
    ag_s, ag_r, a2a_s, a2a_r, id_s, id_r, bk_s, bk_r, px_s, px_r, loc,
):
    f = lax.axis_index("fsdp")
    d = lax.axis_index("dp")
    x = f // 4
    y = lax.rem(f, 4)

    def member(r):
        return lax.rem(x + r // 4, 2) * 4 + lax.rem(y + r % 4, 4)

    def back(r):
        return lax.rem(x + r // 4, 2) * 4 + lax.rem(y + 4 - r % 4, 4)

    width = 1 << bit
    partner = d + width - 2 * width * lax.rem(d // width, 2)
    to_partner = {"dp": partner}

    def rows(block, start=0, size=128):
        return pl.ds(pl.multiple_of(block * 128 + start, 16), size)

    def head_cols(block, h):
        return pl.ds(pl.multiple_of(block * 256 + h * 128, 128), 128)

    def remote(src, dst, s_sem, r_sem, device):
        return pltpu.make_async_remote_copy(
            src_ref=src, dst_ref=dst, send_sem=s_sem, recv_sem=r_sem, device_id=device, device_id_type=MESH
        )

    own_rows = rows(f)
    arrays = ((q, qb), (k, kb), (v, vb))
    results = ((dqb, dq), (dkb, dk), (dvb, dv))
    quarters = [pl.ds(64 * n, 64) for n in range(4)]
    in_p = [pltpu.make_async_copy(params.at[part, :], pf.at[part, :], loc.at[10 + n]) for n, part in enumerate(quarters)]
    in_bm = pltpu.make_async_copy(bm_in, bm, loc.at[14])
    in_step = pltpu.make_async_copy(step_in, step, loc.at[0])
    in_m = pltpu.make_async_copy(mom, mf, loc.at[1])
    in_id = pltpu.make_async_copy(ids, idb.at[f], loc.at[2])
    in_og = pltpu.make_async_copy(og, ogb.at[own_rows, :], loc.at[3])

    def in_head(n, h):
        src, dst = arrays[n]
        return pltpu.make_async_copy(src.at[:, head_cols(f, h)], dst.at[h, own_rows, :], loc.at[4 + 2 * n + h])

    barrier = pltpu.get_barrier_semaphore()
    for r in range(1, 8):
        pl.semaphore_signal(barrier, inc=1, device_id={"fsdp": member(r)}, device_id_type=MESH)
    pl.semaphore_signal(barrier, inc=1, device_id=to_partner, device_id_type=MESH)
    for copy in (*in_p, in_id, in_bm, in_og, in_m, in_step):
        copy.start()
    for n in range(3):
        for h in range(2):
            in_head(n, h).start()

    pl.semaphore_wait(barrier, 8)

    n_x = {"fsdp": member(4)}
    y_p = {"fsdp": member(1)}
    y_m = {"fsdp": member(3)}
    all_rows = (0, 128)
    all_cols = (0, INNER)

    def gather(n, block, span, cols, device):
        part = ogb.at[rows(block, *span), pl.ds(cols[0], cols[1])]
        return remote(og if n < 3 else part, part, ag_s.at[n], ag_r.at[n], device)

    gathers = [
        (0, 0, all_rows, all_cols, n_x), (1, 0, all_rows, all_cols, y_p), (2, 0, all_rows, all_cols, y_m),
        (3, 1, (0, 64), all_cols, y_m), (4, 3, (64, 64), all_cols, y_p),
        (5, 4, all_rows, (0, top), y_p), (6, 4, all_rows, (0, top), y_m),
        (7, 1, all_rows, (top, INNER - top), n_x), (8, 3, all_rows, (top, INNER - top), n_x),
        (9, 2, all_rows, (top, INNER - top), n_x),
        (10, 7, (64, 64), (0, top), y_p), (11, 5, (0, 64), (0, top), y_m),
    ]
    lands = (4, 3, 1, 2, 2, 7, 5, 5, 7, 6, 6, 6)
    live = [n for n in range(12) if top < INNER or n not in (7, 8, 9)]

    def gather_send(*which):
        for n in which:
            if n in live:
                _, r, span, cols, device = gathers[n]
                gather(n, member(r), span, cols, device).start()

    def gather_wait(*which):
        for n in which:
            if n in live:
                _, _, span, cols, device = gathers[n]
                gather(n, member(lands[n]), span, cols, device).wait_recv()

    def exchange(n, h, r):
        src, dst = arrays[n]
        g = member(r)
        return remote(
            src.at[:, head_cols(g, h)], dst.at[h, own_rows, :], a2a_s.at[h, n, r], a2a_r.at[h, n, r], {"fsdp": g}
        )

    def give_back(n, h, r):
        src, dst = results[n]
        g = member(r)
        return remote(
            src.at[h, rows(g), :], dst.at[:, head_cols(f, h)], bk_s.at[h, n, r], bk_r.at[h, n, r], {"fsdp": g}
        )

    def keep_back(n, h):
        src, dst = results[n]
        return pltpu.make_async_copy(src.at[h, own_rows, :], dst.at[:, head_cols(f, h)], loc.at[4 + 2 * n + h])

    def swap_m(h, n):
        part = (pl.ds(pl.multiple_of(h * 128, 128), 128), pl.ds(pl.multiple_of(n * 256, 256), 256))
        return remote(m16.at[part], mr.at[part], px_s.at[1 + h * 8 + n], px_r.at[1 + h * 8 + n], to_partner)

    for r in range(1, 8):
        remote(ids, idb.at[f], id_s.at[r], id_r.at[r], {"fsdp": member(r)}).start()
    gather_send(0, 1, 2)

    def exchange_first():
        for n in range(3):
            for r in range(1, 8):
                exchange(n, 0, r).start()

    def swap_p(n):
        part = quarters[n]
        return remote(w16.at[part, :], pr.at[part, :], px_s.at[17 + n], px_r.at[17 + n], to_partner)

    if bit == 1:
        exchange_first()
    for n, part in enumerate(quarters):
        in_p[n].wait()
        w16[part, :] = pf[part, :].astype(BF)
        if n:
            swap_p(n - 1).start()
    if bit != 1:
        exchange_first()
    swap_p(3).start()
    in_m.wait()
    in_id.wait()
    in_bm.wait()
    in_step.wait()
    for r in range(1, 8):
        remote(ids, idb.at[back(r)], id_s.at[r], id_r.at[r], n_x).wait_recv()

    def stem_col(g, _):
        stem = lax.shift_right_logical(idb[g], 11).astype(F32)
        spread = jnp.broadcast_to(stem, (128, 128))
        skc[pl.ds(pl.multiple_of(g * 128, 128), 128), :] = spread.T
        return 0

    lax.fori_loop(0, 8, stem_col, 0)

    iota_k = lax.broadcasted_iota(jnp.int32, (128, 128), 0)
    iota_q = lax.broadcasted_iota(jnp.int32, (128, 128), 1)
    tri = jnp.where(iota_k <= iota_q, 0.0, NEG).astype(F32)

    def bias_row(kg, _):
        k_rows = pl.ds(pl.multiple_of(kg * 128, 128), 128)
        sk = skc[k_rows, :]
        bias[k_rows, k_rows] = tri

        def bias_tile(qg, _):
            sq = lax.shift_right_logical(idb[qg], 11).astype(F32)
            sq = sq + (1 - bm[qg, kg]).astype(F32) * 16.0
            bias[k_rows, pl.ds(pl.multiple_of(qg * 128, 128), 128)] = jnp.where(sk == sq, 0.0, NEG)
            return 0

        lax.fori_loop(kg + 1, 8, bias_tile, 0)
        return 0

    lax.fori_loop(0, 8, bias_row, 0)
    for ip in range(4):
        bias[256 * ip + 128 : 256 * ip + 256, 256 * ip : 256 * ip + 128] = jnp.full((128, 128), NEG, F32)

    inv_width = 1.0 / math.sqrt(INNER)
    scale = 1.0 / math.sqrt(HD)
    scale2 = scale * math.log2(math.e)

    def grad_block(block):
        at = rows(block)
        grad = (dot(ogb[at, :], w16[...], CT_MINOR) * inv_width).astype(BF)
        gr[0, at, :] = grad[:, :HD]
        gr[1, at, :] = grad[:, HD:]

    in_og.wait()
    grad_block(f)
    gather_wait(0, 1, 2)
    gather_send(3, 4, 5, 6, 7, 8)
    for r in (4, 1, 3):
        grad_block(member(r))

    def forward(h, ip):
        size = 256 * (ip + 1)
        here = slice(256 * ip, 256 * ip + 256)
        s = dot(kb[h, 0:size, :], qb[h, here, :], CT_MINOR) * scale2 + bias[0:size, here]
        e = jnp.exp2(s - jnp.max(s, axis=0, keepdims=True))
        p = (e * (1.0 / jnp.sum(e, axis=0, keepdims=True))).astype(BF)
        pt[0:size, here] = p
        att[h, :, here] = dot(vb[h, 0:size, :], p, CT_MAJOR).astype(BF)

    def backward(h, ip):
        size = 256 * (ip + 1)
        here = slice(256 * ip, 256 * ip + 256)
        g = gr[h, here, :]
        p16 = pt[0:size, here]
        p = p16.astype(F32)
        dp = dot(vb[h, 0:size, :], g, CT_MINOR)
        row_dot = jnp.sum(p * dp, axis=0, keepdims=True)
        ds = (p * (dp - row_dot) * scale).astype(BF)
        dv_part = dot(p16, g, CT_PLAIN)
        dk_part = dot(ds, qb[h, here, :], CT_PLAIN)
        if ip == 3:
            dva[0:size, :] = dv_part
            dka[0:size, :] = dk_part
        else:
            dva[0:size, :] += dv_part
            dka[0:size, :] += dk_part
        dqb[h, here, :] = dot(ds, kb[h, 0:size, :], CT_MAJOR).astype(BF)

    def one_head(h, _):
        for n in range(3):
            in_head(n, h).wait()
            for r in range(1, 8):
                land = arrays[n][1].at[h, rows(back(r)), :]
                remote(land, land, a2a_s.at[h, n, r], a2a_r.at[h, n, r], n_x).wait_recv()
        for ip in range(4):
            forward(h, ip)

        @pl.when(h == 0)
        def _():
            gather_wait(3, 4)
            gather_send(9)
            for r in (1, 2, 3):
                exchange(0, 1, r).start()
            grad_block(member(2))
            gather_wait(5, 6)
            gather_send(10, 11)
            for n in range(3):
                for r in range(4 if n == 0 else 1, 8):
                    exchange(n, 1, r).start()
            gather_wait(7, 8)
            grad_block(member(5))
            grad_block(member(7))
            gather_wait(9, 10, 11)
            grad_block(member(6))

        def weight():
            h_rows = pl.ds(pl.multiple_of(h * 128, 128), 128)

            def weight_cols(n, _):
                cols = pl.ds(pl.multiple_of(n * 256, 256), 256)
                moment = MOMENTUM_RATE * mf[h_rows, cols] + dot(att[h], ogb[:, cols], CT_PLAIN) * inv_width
                mf[h_rows, cols] = moment
                m16[h_rows, cols] = moment.astype(BF)

                @pl.when(n > 0)
                def _():
                    swap_m(h, n - 1).start()

                return 0

            lax.fori_loop(0, 8, weight_cols, 0)
            swap_m(h, 7).start()

        def finish(n, _):
            part = pl.ds(pl.multiple_of(n * 128, 128), 128)
            dkb[h, part, :] = dka[part, :].astype(BF)
            dvb[h, part, :] = dva[part, :].astype(BF)
            return 0

        if bit in (1, 2):
            weight()
        for ip in (3, 2, 1, 0):
            backward(h, ip)
        lax.fori_loop(0, 8, finish, 0)
        for n in range(3):
            for r in range(1, 8):
                give_back(n, h, r).start()
            keep_back(n, h).start()
        if bit in (0, 3):
            weight()
        return 0

    lax.fori_loop(0, 2, one_head, 0)

    for r in range(1, 8):
        remote(ids, idb.at[f], id_s.at[r], id_r.at[r], n_x).wait_send()
    for n in live:
        _, r, span, cols, device = gathers[n]
        gather(n, member(r), span, cols, device).wait_send()

    def drain_back(h):
        for n in range(3):
            for r in range(1, 8):
                exchange(n, h, r).wait_send()
                give_back(n, h, r).wait_send()
                land = results[n][1].at[:, head_cols(back(r), h)]
                remote(land, land, bk_s.at[h, n, r], bk_r.at[h, n, r], n_x).wait_recv()
            keep_back(n, h).wait()

    power = jnp.exp((jnp.zeros((8, 128), jnp.int32) + (step[0] + 1)).astype(F32) * math.log(MOMENTUM_RATE))
    rate = (LEARN_RATE * (1.0 / (1.0 - power)))[0:1, 0:1]

    def drain_m(h):
        part = pl.ds(h * 128, 128)

        def average(n, _):
            swap_m(h, n).wait()
            cols = pl.ds(pl.multiple_of(n * 256, 256), 256)
            momentum = 0.5 * (mf[part, cols] + mr[part, cols].astype(F32))
            mf[part, cols] = momentum
            pf[part, cols] = 0.5 * (pf[part, cols] + pr[part, cols].astype(F32)) - rate * momentum
            return 0

        lax.fori_loop(0, 8, average, 0)

    for n in range(4):
        swap_p(n).wait()
    drain_m(0)
    drain_back(0)
    if bit == 0:
        drain_m(1)
    drain_back(1)
    if bit != 0:
        drain_m(1)


def fused(bit, step, bm, q, k, v, og, params, mom, ids):
    anyspace = pl.BlockSpec(memory_space=pl.ANY)
    vmem = pl.BlockSpec(memory_space=pltpu.VMEM)
    tok = jax.ShapeDtypeStruct((128, INNER), BF)
    full = jax.ShapeDtypeStruct((256, INNER), F32)
    half = pltpu.VMEM((256, INNER), BF)
    dma = pltpu.SemaphoreType.DMA
    heads = pltpu.VMEM((2, 1024, 128), BF)
    return pl.pallas_call(
        functools.partial(kernel, bit, INNER if bit == 1 else 1152),
        name=f"step_{bit}",
        out_shape=(tok, tok, tok, full, full),
        in_specs=[anyspace] * 9,
        out_specs=(vmem,) * 5,
        scratch_shapes=[
            pltpu.SMEM((1,), jnp.int32),
            pltpu.SMEM((8, 8), jnp.int32),
            half, half,
            heads, heads, heads,
            pltpu.VMEM((1024, INNER), BF),
            pltpu.VMEM((256, INNER), BF),
            pltpu.VMEM((256, INNER), BF),
            pltpu.VMEM((8, 1, 128), jnp.int32),
            pltpu.VMEM((1024, 128), F32),
            pltpu.VMEM((1024, 1024), F32),
            pltpu.VMEM((1024, 1024), BF),
            pltpu.VMEM((2, 128, 1024), BF),
            heads, heads, heads, heads,
            pltpu.VMEM((1024, 128), F32),
            pltpu.VMEM((1024, 128), F32),
            dma((12,)), dma((12,)), dma((2, 3, 8)), dma((2, 3, 8)), dma((8,)), dma((8,)),
            dma((2, 3, 8)), dma((2, 3, 8)), dma((21,)), dma((21,)), dma((15,)),
        ],
        compiler_params=pltpu.CompilerParams(
            collective_id=bit, has_side_effects=True, vmem_limit_bytes=46 * 1024 * 1024
        ),
    )(step, bm, q, k, v, og, params, mom, ids)


def finish_kernel(*refs):
    copies = []
    for n in range(5):
        src, dst = refs[n], refs[5 + n]
        size = src.shape[0] // 4
        for m in range(4):
            part = pl.ds(m * size, size)
            copies.append(pltpu.make_async_copy(src.at[part, :], dst.at[part, :], refs[10].at[n, m]))
            copies[-1].start()
    for copy in copies:
        copy.wait()


def finish_call(*parts):
    anyspace = pl.BlockSpec(memory_space=pl.ANY)
    vmem = pl.BlockSpec(memory_space=pltpu.VMEM)
    return pl.pallas_call(
        finish_kernel,
        name="finish",
        out_shape=tuple(jax.ShapeDtypeStruct(part.shape, part.dtype) for part in parts),
        in_specs=[vmem] * 5,
        out_specs=(anyspace,) * 5,
        scratch_shapes=[pltpu.SemaphoreType.DMA((5, 4))],
        compiler_params=pltpu.CompilerParams(vmem_limit_bytes=16 * 1024 * 1024),
    )(*parts)


def shards(q, k, v, og, params, mom, token_ids, block_mask, step_index):
    ids = token_ids.reshape(1, 128)


    def branch(bit):
        def run(*parts):
            return finish_call(*fused(bit, *parts))

        return run

    return lax.switch(
        step_index[0] & 3,
        [branch(bit) for bit in range(4)],
        step_index, block_mask, q, k, v, og, params, mom, ids,
    )


def solution(mesh):
    split = P(("dp", "fsdp"), None)
    return jax.shard_map(
        shards,
        mesh=mesh,
        in_specs=(split,) * 6 + (P(("dp", "fsdp")), P(), P()),
        out_specs=(split,) * 5,
        check_vma=False,
    )
```
